256 devices in a mesh: op: 32 (over z_lo, x, core), term: 8 (over z_hi, y).
Axes of the slice: x: 4, y: 4, z: 8 (z_hi: 2, z_lo: 4; z = z_hi * 4 + z_lo), core: 2. Of those that a mesh axis runs over, the one named last changes fastest.
Arguments:
- wavefunction: float32 [32, 384, 384], P('op'), may hold values from -6 to 6
- left_dims: int32 [32], P('op'), may hold values from 192 to 384
- right_dims: int32 [32], P('op'), may hold values from 192 to 384
- left_operators: float32 [32, 8, 384, 384], P('op', 'term'), may hold values from -0.109375 to 0.109375
- right_operators: float32 [32, 8, 384, 384], P('op', 'term'), may hold values from -0.3125 to 0.3125
- charges: int32 [32, 8], P('op', 'term'), may hold values from 0 to 11
Outputs:
- applied: float32 [32, 384, 384], P('op', 'term')
The draws below stay inside these ranges and needn't reach their ends.
Inputs may be any that keep to these rules, and one draw needn't show every extreme that they name: `charges`: a term of source sector s acts into sector (s + charge) mod 32.
All inputs are finite; a program needn't handle non-finite values.
Results may differ from the reference program's by a relative error of at most 0.0003.
Values sent between devices are 32-bit elements; how exact they have to be, the bound alone decides.
A program may use at most 64 MiB of HBM per device.

```python
import jax
import jax.numpy as jnp
from jax import lax

B = 384
CHARGES = 12
SECTORS = 32
TPT = 8


def place_ends(values, rng, smallest, top_value):
    dims = values.shape
    spot = [jax.random.randint(jax.random.fold_in(rng, axis), (), 0, dims[axis]) for axis in range(len(dims))]
    values = values.at[tuple(spot)].set(smallest)
    longest = dims.index(max(dims))
    spot[longest] = (spot[longest] + 1) % dims[longest]
    return values.at[tuple(spot)].set(top_value)


def level_of(key, dims, shards, least, top_value):
    loudness, own = 1.0, jax.random.fold_in(key, 6)
    for dim, parts in shards:
        draws = jnp.exp(jax.random.uniform(jax.random.fold_in(own, dim), (parts,), jnp.float32, least / len(shards), top_value / len(shards)))
        loudness = loudness * jnp.repeat(draws, dims[dim] // parts).reshape([-1 if axis == dim else 1 for axis in range(len(dims))])
    return loudness


def scatter_about(own_key, shape, deviation, most, split=(), kind=jnp.bfloat16):
    factor_of = level_of(own_key, shape, split, -0.22, 0.18) if split else 1.0
    array = jax.random.normal(own_key, shape, jnp.float32) * deviation * factor_of
    return jnp.minimum(jnp.maximum(array, -most), most).astype(kind)


def setup_inputs(seed: int = 0) -> dict:
    arg_keys = jax.random.split(jax.random.key(seed), 7)
    wavefunction = scatter_about(arg_keys[0], (SECTORS, B, B), 1.0, 6.0, ((0, 32),), jnp.float32)
    left_dims = place_ends(jax.random.randint(arg_keys[1], (SECTORS,), B // 2, B + 1), jax.random.fold_in(arg_keys[1], 1), B // 2, B).astype(jnp.int32)
    right_dims = place_ends(jax.random.randint(arg_keys[2], (SECTORS,), B // 2, B + 1), jax.random.fold_in(arg_keys[2], 1), B // 2, B).astype(jnp.int32)
    left_operators = scatter_about(arg_keys[3], (SECTORS, TPT, B, B), (B * TPT) ** -0.5, 0.109375, ((0, 32), (1, 8)), jnp.float32)
    right_operators = scatter_about(arg_keys[4], (SECTORS, TPT, B, B), B ** -0.5, 0.3125, ((0, 32), (1, 8)), jnp.float32)
    charges = place_ends(jax.random.randint(arg_keys[5], (SECTORS, TPT), 0, CHARGES), jax.random.fold_in(arg_keys[5], 1), 0, CHARGES - 1).astype(jnp.int32)
    return {"wavefunction": wavefunction, "left_dims": left_dims, "right_dims": right_dims, "left_operators": left_operators, "right_operators": right_operators, "charges": charges}


TOP_CHARGE = lax.Precision.HIGHEST


def reference(wavefunction, left_dims, right_dims, left_operators, right_operators, charges):
    positions = jnp.arange(B).astype(jnp.int32)
    live_mask = ((positions[None, :, None] < left_dims[:, None, None]) & (positions[None, None, :] < right_dims[:, None, None])).astype(jnp.float32)
    mask_applied = wavefunction * live_mask
    sectors = jnp.arange(SECTORS).astype(jnp.int32)

    def one_sector(carried, sector_items):
        incoming_block, left_term_stack, right_term_stack, term_charge, source = sector_items
        left_product = jnp.einsum("ims,sd->imd", left_term_stack, incoming_block, precision=TOP_CHARGE)
        term_contribution = jnp.einsum("opu,oru->opr", left_product, right_term_stack, precision=TOP_CHARGE)
        targets = (source + term_charge) % SECTORS
        one_hot = (sectors[:, None] == targets[None, :]).astype(jnp.float32)
        return carried + jnp.einsum("kt,tab->kab", one_hot, term_contribution, precision=TOP_CHARGE), source

    summed, unused = lax.scan(one_sector, jnp.zeros((SECTORS, B, B), jnp.float32), (mask_applied, left_operators, right_operators, charges, sectors))
    return summed * live_mask
```

```python
import jax
import jax.numpy as jnp
from jax import lax
from jax.sharding import PartitionSpec as P

CHARGES = 12
TOP_CHARGE = lax.Precision.HIGHEST


def shifted(value, axis, steps):
    count = lax.axis_size(axis)
    pairs = [(source, (source + steps) % count) for source in range(count)]
    return lax.ppermute(value, axis, pairs)


def on_device(wavefunction, left_dims, right_dims, left_operators, right_operators, charges):
    block_order = wavefunction.shape[1]
    positions = jnp.arange(block_order)
    peers = lax.axis_size("term")
    rows = block_order // peers
    mask_applied = wavefunction[0] * (
        (positions[:, None] < left_dims[0]) & (positions[None, :] < right_dims[0])
    ).astype(jnp.float32)
    left_product = jnp.einsum("ims,sd->imd", left_operators[0], mask_applied, precision=TOP_CHARGE)
    contribution = jnp.einsum(
        "opu,oru->opr", left_product, right_operators[0], precision=TOP_CHARGE
    )[0]
    tag = jnp.broadcast_to(charges.astype(jnp.float32)[:, :, None], (peers, 8, block_order))
    pieces = jnp.concatenate([contribution.reshape(peers, rows, block_order), tag], axis=1)
    arrived = lax.all_to_all(pieces, "term", split_axis=0, concat_axis=0, tiled=True)
    blocks, tags = arrived[:, :rows], arrived[:, rows, 0]

    def charge_part(charge_value):
        chosen = (tags == charge_value)[:, None, None]
        return jnp.where(chosen, blocks, 0.0).sum(axis=0)

    summed = charge_part(CHARGES - 1)
    for charge_value in range(CHARGES - 2, -1, -1):
        summed = shifted(summed, "op", 1) + charge_part(charge_value)
    row_index = lax.axis_index("term") * rows + jnp.arange(rows)
    live_rows = ((row_index[:, None] < left_dims[0]) & (positions[None, :] < right_dims[0])).astype(
        jnp.float32
    )
    return (summed * live_rows)[None]


def solution(mesh):
    in_specs = (
        P("op", None, None),
        P("op"),
        P("op"),
        P("op", "term", None, None),
        P("op", "term", None, None),
        P("op", "term"),
    )
    out_specs = P("op", "term", None)
    return jax.shard_map(
        on_device, mesh=mesh, in_specs=in_specs, out_specs=out_specs, check_vma=False
    )
```

```python
import functools

import jax
import jax.numpy as jnp
from jax import lax
from jax.experimental import pallas as pl
from jax.experimental.pallas import tpu as pltpu
from jax.sharding import PartitionSpec as P

B = 384
ROWS = 48
PIECES = 8
CHUNKS = 3
STEP = ROWS // CHUNKS
TARGETS = 13
MESH = pl.DeviceIdType.MESH
F32, BF16 = jnp.float32, jnp.bfloat16

SHIFT_TARGETS = ((0, 1, 8, 9), (2, 3, 10, 11), (4, 5, 12), (6, 7))
SHIFT_START = (0, 4, 8, 11)
PLACE = {t: SHIFT_START[s] + i for s, group in enumerate(SHIFT_TARGETS) for i, t in enumerate(group)}


def halves(value):
    high = value.astype(BF16)
    return high, (value - high.astype(F32)).astype(BF16)


def dot3(a, b, contract):
    dims = (contract, ((), ()))
    one = functools.partial(lax.dot_general, dimension_numbers=dims, preferred_element_type=F32)
    return one(a[0], b[0]) + (one(a[0], b[1]) + one(a[1], b[0]))


def kernel(
    left_dims, right_dims, charges, wave_hbm, left_hbm, right_hbm, out,
    wave, left, right, tag_out, tag_in, y_out, y_in, x_out, x_in, z_out, z_in,
    in_sem, tag_ss, tag_rs, y_ss, y_rs, x_ss, x_rs, z_ss, z_rs,
):
    op, term = lax.axis_index("op"), lax.axis_index("term")
    core, x, z_lo = op % 2, (op // 2) % 4, op // 8
    y, z_hi = term % 4, term // 4
    far = (z_hi != core).astype(jnp.int32)

    def device(z_lo_, x_, core_, z_hi_, y_):
        return {"op": (z_lo_ * 4 + x_) * 2 + core_, "term": z_hi_ * 4 + y_}

    def y_peer(slot):
        return device(z_lo, x, (core + slot) % 2, z_hi, (y + 4 - slot // 2) % 4)

    def y_source(slot):
        return device(z_lo, x, (core + slot) % 2, z_hi, (y + slot // 2) % 4)

    loads = [
        pltpu.make_async_copy(wave_hbm, wave, in_sem.at[0]),
        pltpu.make_async_copy(left_hbm, left, in_sem.at[1]),
        pltpu.make_async_copy(right_hbm, right, in_sem.at[2]),
    ]
    for load in loads:
        load.start()

    barrier = pltpu.get_barrier_semaphore()

    def greet(device_id):
        pl.semaphore_signal(barrier, inc=1, device_id=device_id, device_id_type=MESH)

    for slot in range(1, PIECES):
        greet(y_source(slot))
    for shift in range(1, 4):
        greet(device(z_lo, (x + 4 - shift) % 4, core, z_hi, y))
    for ahead in range(3):
        for half in range(2):
            source = device((z_lo + 4 - ahead) % 4, x, z_hi, (z_hi + half) % 2, y)
            if ahead == 0 and half == 0:
                pl.when(far == 1)(functools.partial(greet, source))
            else:
                greet(source)

    tag_out[...] = jnp.full((8, 128), charges[0, 0] + core, jnp.int32)
    tag_in[0] = tag_out[...]

    loads[0].wait()
    live = (lax.broadcasted_iota(jnp.int32, (B, B), 0) < left_dims[0]) & (
        lax.broadcasted_iota(jnp.int32, (B, B), 1) < right_dims[0]
    )
    wave_parts = halves(jnp.where(live, wave[...], 0.0))
    loads[2].wait()
    right_parts = halves(right[...])
    loads[1].wait()

    def contribution(chunk):
        rows = left[:, chunk * STEP : (chunk + 1) * STEP, :].reshape(PIECES * STEP, B)
        product = dot3(halves(rows), wave_parts, ((1,), (0,)))
        result = dot3(halves(product), right_parts, ((1,), (1,)))
        y_out[chunk] = result.reshape(PIECES, STEP, B)

    def y_copy(chunk, slot):
        peer = y_peer(slot)
        piece = (core + slot) % 2 * 4 + (y + 4 - slot // 2) % 4
        return pltpu.make_async_remote_copy(
            src_ref=y_out.at[chunk, piece],
            dst_ref=y_in.at[chunk, slot],
            send_sem=y_ss.at[chunk, slot],
            recv_sem=y_rs.at[chunk, slot],
            device_id=peer,
            device_id_type=MESH,
        )

    def tag_copy(slot):
        return pltpu.make_async_remote_copy(
            src_ref=tag_out,
            dst_ref=tag_in.at[slot],
            send_sem=tag_ss.at[slot],
            recv_sem=tag_rs.at[slot],
            device_id=y_peer(slot),
            device_id_type=MESH,
        )

    def x_copy(chunk, shift):
        size = len(SHIFT_TARGETS[shift])
        return pltpu.make_async_remote_copy(
            src_ref=x_out.at[chunk, pl.ds(SHIFT_START[shift], size)],
            dst_ref=x_in.at[chunk, pl.ds(SHIFT_START[shift] - 4, size)],
            send_sem=x_ss.at[chunk, shift],
            recv_sem=x_rs.at[chunk, shift],
            device_id=device(z_lo, (x + shift) % 4, core, z_hi, y),
            device_id_type=MESH,
        )

    def z_copy(chunk, ahead, other):
        target_core = (core + other) % 2
        return pltpu.make_async_remote_copy(
            src_ref=z_out.at[chunk, ahead, target_core],
            dst_ref=z_in.at[chunk, ahead * 2 + far],
            send_sem=z_ss.at[chunk, ahead * 2 + other],
            recv_sem=z_rs.at[chunk, ahead * 2 + far],
            device_id=device((z_lo + ahead) % 4, x, target_core, core, y),
            device_id_type=MESH,
        )

    def z_arrival(chunk, slot):
        return pltpu.make_async_remote_copy(
            src_ref=z_out.at[chunk, 0, 0],
            dst_ref=z_in.at[chunk, slot],
            send_sem=z_ss.at[chunk, slot],
            recv_sem=z_rs.at[chunk, slot],
            device_id=device(z_lo, x, (core + 1) % 2, z_hi, y),
            device_id_type=MESH,
        )

    y_order = (4, 5, 2, 3, 6, 7, 1)

    for chunk in range(CHUNKS):
        contribution(chunk)
        if chunk == 0:
            pl.semaphore_wait(barrier, 15 + far)
            for slot in y_order:
                tag_copy(slot).start()
        for slot in y_order:
            y_copy(chunk, slot).start()

    for chunk in range(CHUNKS):
        if chunk == 0:
            for slot in range(1, PIECES):
                tag_copy(slot).wait_recv()
        y_in[chunk, 0] = y_out[chunk, core * 4 + y]
        for slot in range(1, PIECES):
            y_copy(chunk, slot).wait_recv()
        tags = [tag_in[slot] for slot in range(PIECES)]
        for row in range(0, STEP, 8):
            for column in range(0, B, 128):
                spot = (slice(row, row + 8), slice(column, column + 128))
                blocks = [y_in[(chunk, slot) + spot] for slot in range(PIECES)]
                for target in range(TARGETS):
                    parts = [jnp.where(t == target, b, 0.0) for t, b in zip(tags, blocks)]
                    while len(parts) > 1:
                        parts = [a + b for a, b in zip(parts[::2], parts[1::2])]
                    x_out[(chunk, PLACE[target]) + spot] = parts[0]
        for shift in (2, 1, 3):
            x_copy(chunk, shift).start()

    for chunk in range(CHUNKS):
        for shift in range(1, 4):
            x_copy(chunk, shift).wait_recv()
        for q in range(2):
            first = [x_in[chunk, SHIFT_START[s] - 4 + q] for s in (1, 2, 3)]
            second = [x_in[chunk, 2 + q], x_in[chunk, 6] if q == 0 else None]
            near = [x >= s for s in (1, 2, 3)]
            sums = [x_out[chunk, q], x_out[chunk, 2 + q], jnp.zeros((STEP, B), F32)]
            for is_near, block in zip(near, first):
                sums[0] += jnp.where(is_near, block, 0.0)
                sums[1] += jnp.where(is_near, 0.0, block)
            for is_near, block in zip(near, second):
                if block is not None:
                    sums[1] += jnp.where(is_near, block, 0.0)
                    sums[2] += jnp.where(is_near, 0.0, block)
            for ahead in range(3):
                z_out[chunk, ahead, q] = sums[ahead]

        for ahead, other in ((0, 0), (0, 1), (1, 0), (1, 1), (2, 0), (2, 1)):
            if ahead == 0 and other == 0:

                @pl.when(far == 1)
                def _():
                    z_copy(chunk, 0, 0).start()

                @pl.when(far == 0)
                def _():
                    z_in[chunk, 0] = z_out[chunk, 0, core]
            else:
                z_copy(chunk, ahead, other).start()

    for chunk in range(CHUNKS):
        for slot in range(6):
            if slot == 0:

                @pl.when(far == 1)
                def _():
                    z_arrival(chunk, 0).wait_recv()
            else:
                z_arrival(chunk, slot).wait_recv()
        blocks = [z_in[chunk, slot] for slot in range(6)]
        total = (blocks[0] + blocks[1]) + (blocks[2] + blocks[3]) + (blocks[4] + blocks[5])
        out[chunk * STEP : (chunk + 1) * STEP, :] = total

    for slot in range(1, PIECES):
        tag_copy(slot).wait_send()
    for chunk in range(CHUNKS):
        for slot in range(1, PIECES):
            y_copy(chunk, slot).wait_send()
        for shift in range(1, 4):
            x_copy(chunk, shift).wait_send()
        for ahead in range(3):
            for other in range(2):
                if ahead == 0 and other == 0:

                    @pl.when(far == 1)
                    def _():
                        z_copy(chunk, 0, 0).wait_send()
                else:
                    z_copy(chunk, ahead, other).wait_send()


def on_device(wavefunction, left_dims, right_dims, left_operators, right_operators, charges):
    smem = pl.BlockSpec(memory_space=pltpu.SMEM)
    hbm = pl.BlockSpec(memory_space=pl.ANY)
    dma = pltpu.SemaphoreType.DMA
    summed = pl.pallas_call(
        kernel,
        out_shape=jax.ShapeDtypeStruct((ROWS, B), F32),
        in_specs=[smem, smem, smem, hbm, hbm, hbm],
        out_specs=pl.BlockSpec(memory_space=pltpu.VMEM),
        scratch_shapes=[
            pltpu.VMEM((B, B), F32),
            pltpu.VMEM((PIECES, ROWS, B), F32),
            pltpu.VMEM((B, B), F32),
            pltpu.VMEM((8, 128), jnp.int32),
            pltpu.VMEM((PIECES, 8, 128), jnp.int32),
            pltpu.VMEM((CHUNKS, PIECES, STEP, B), F32),
            pltpu.VMEM((CHUNKS, PIECES, STEP, B), F32),
            pltpu.VMEM((CHUNKS, TARGETS, STEP, B), F32),
            pltpu.VMEM((CHUNKS, TARGETS - 4, STEP, B), F32),
            pltpu.VMEM((CHUNKS, 3, 2, STEP, B), F32),
            pltpu.VMEM((CHUNKS, 6, STEP, B), F32),
            dma((3,)),
            dma((PIECES,)),
            dma((PIECES,)),
            dma((CHUNKS, PIECES)),
            dma((CHUNKS, PIECES)),
            dma((CHUNKS, 4)),
            dma((CHUNKS, 4)),
            dma((CHUNKS, 6)),
            dma((CHUNKS, 6)),
        ],
        compiler_params=pltpu.CompilerParams(collective_id=0, has_side_effects=True),
        name="sector_scatter",
    )(
        left_dims,
        right_dims,
        charges,
        wavefunction[0],
        left_operators.reshape(PIECES, ROWS, B),
        right_operators[0, 0],
    )
    row_index = lax.axis_index("term") * ROWS + jnp.arange(ROWS)
    live_rows = ((row_index[:, None] < left_dims[0]) & (jnp.arange(B)[None, :] < right_dims[0])).astype(F32)
    return (summed * live_rows)[None]


def solution(mesh):
    in_specs = (
        P("op", None, None),
        P("op"),
        P("op"),
        P("op", "term", None, None),
        P("op", "term", None, None),
        P("op", "term"),
    )
    out_specs = P("op", "term", None)
    return jax.shard_map(
        on_device, mesh=mesh, in_specs=in_specs, out_specs=out_specs, check_vma=False
    )
```

```python
import functools

import jax
import jax.numpy as jnp
from jax import lax
from jax.experimental import pallas as pl
from jax.experimental.pallas import tpu as pltpu
from jax.sharding import PartitionSpec as P

B = 384
ROWS = 48
PIECES = 8
CHUNKS = 6
STEP = ROWS // CHUNKS
TARGETS = 13
MESH = pl.DeviceIdType.MESH
F32, BF16 = jnp.float32, jnp.bfloat16

SHIFT_TARGETS = ((0, 1, 8, 9), (2, 3, 10, 11), (4, 5, 12), (6, 7))
SHIFT_START = (0, 4, 8, 11)
PLACE = {t: SHIFT_START[s] + i for s, group in enumerate(SHIFT_TARGETS) for i, t in enumerate(group)}


def halves(value):
    high = value.astype(BF16)
    return high, (value - high.astype(F32)).astype(BF16)


def dot3(a, b, contract):
    dims = (contract, ((), ()))
    one = functools.partial(lax.dot_general, dimension_numbers=dims, preferred_element_type=F32)
    return one(a[0], b[0]) + (one(a[0], b[1]) + one(a[1], b[0]))


def kernel(
    left_dims, right_dims, charges, wave_hbm, left_hbm, right_hbm, out,
    wave, left, right, tag_out, tag_in, y_out, y_in, x_out, x_in, z_out, z_in,
    in_sem, tag_ss, tag_rs, y_ss, y_rs, x_ss, x_rs, z_ss, z_rs,
):
    op, term = lax.axis_index("op"), lax.axis_index("term")
    core, x, z_lo = op % 2, (op // 2) % 4, op // 8
    y, z_hi = term % 4, term // 4
    far = (z_hi != core).astype(jnp.int32)

    def device(z_lo_, x_, core_, z_hi_, y_):
        return {"op": (z_lo_ * 4 + x_) * 2 + core_, "term": z_hi_ * 4 + y_}

    def y_peer(slot):
        return device(z_lo, x, (core + slot) % 2, z_hi, (y + 4 - slot // 2) % 4)

    def y_source(slot):
        return device(z_lo, x, (core + slot) % 2, z_hi, (y + slot // 2) % 4)

    loads = [
        pltpu.make_async_copy(wave_hbm, wave, in_sem.at[0]),
        pltpu.make_async_copy(left_hbm, left, in_sem.at[1]),
        pltpu.make_async_copy(right_hbm, right, in_sem.at[2]),
    ]
    for load in loads:
        load.start()

    barrier = pltpu.get_barrier_semaphore()

    def greet(device_id):
        pl.semaphore_signal(barrier, inc=1, device_id=device_id, device_id_type=MESH)

    for slot in range(1, PIECES):
        greet(y_source(slot))
    for shift in range(1, 4):
        greet(device(z_lo, (x + 4 - shift) % 4, core, z_hi, y))
    for ahead in range(3):
        for half in range(2):
            source = device((z_lo + 4 - ahead) % 4, x, z_hi, (z_hi + half) % 2, y)
            if ahead == 0 and half == 0:
                pl.when(far == 1)(functools.partial(greet, source))
            else:
                greet(source)

    tag_out[...] = jnp.full((8, 128), charges[0, 0] + core, jnp.int32)
    tag_in[0] = tag_out[...]

    loads[0].wait()
    live = (lax.broadcasted_iota(jnp.int32, (B, B), 0) < left_dims[0]) & (
        lax.broadcasted_iota(jnp.int32, (B, B), 1) < right_dims[0]
    )
    wave_parts = halves(jnp.where(live, wave[...], 0.0))
    loads[2].wait()
    right_parts = halves(right[...])
    loads[1].wait()

    def contribution(chunk):
        rows = left[:, chunk * STEP : (chunk + 1) * STEP, :].reshape(PIECES * STEP, B)
        product = dot3(halves(rows), wave_parts, ((1,), (0,)))
        result = dot3(halves(product), right_parts, ((1,), (1,)))
        y_out[chunk] = result.reshape(PIECES, STEP, B)

    def y_copy(chunk, slot):
        peer = y_peer(slot)
        piece = (core + slot) % 2 * 4 + (y + 4 - slot // 2) % 4
        return pltpu.make_async_remote_copy(
            src_ref=y_out.at[chunk, piece],
            dst_ref=y_in.at[chunk, slot],
            send_sem=y_ss.at[chunk, slot],
            recv_sem=y_rs.at[chunk, slot],
            device_id=peer,
            device_id_type=MESH,
        )

    def tag_copy(slot):
        return pltpu.make_async_remote_copy(
            src_ref=tag_out,
            dst_ref=tag_in.at[slot],
            send_sem=tag_ss.at[slot],
            recv_sem=tag_rs.at[slot],
            device_id=y_peer(slot),
            device_id_type=MESH,
        )

    def x_copy(chunk, shift):
        size = len(SHIFT_TARGETS[shift])
        return pltpu.make_async_remote_copy(
            src_ref=x_out.at[chunk, pl.ds(SHIFT_START[shift], size)],
            dst_ref=x_in.at[chunk, pl.ds(SHIFT_START[shift] - 4, size)],
            send_sem=x_ss.at[chunk, shift],
            recv_sem=x_rs.at[chunk, shift],
            device_id=device(z_lo, (x + shift) % 4, core, z_hi, y),
            device_id_type=MESH,
        )

    def z_copy(chunk, ahead, other):
        target_core = (core + other) % 2
        return pltpu.make_async_remote_copy(
            src_ref=z_out.at[chunk, ahead, target_core],
            dst_ref=z_in.at[chunk, ahead * 2 + far],
            send_sem=z_ss.at[chunk, ahead * 2 + other],
            recv_sem=z_rs.at[chunk, ahead * 2 + far],
            device_id=device((z_lo + ahead) % 4, x, target_core, core, y),
            device_id_type=MESH,
        )

    def z_arrival(chunk, slot):
        return pltpu.make_async_remote_copy(
            src_ref=z_out.at[chunk, 0, 0],
            dst_ref=z_in.at[chunk, slot],
            send_sem=z_ss.at[chunk, slot],
            recv_sem=z_rs.at[chunk, slot],
            device_id=device(z_lo, x, (core + 1) % 2, z_hi, y),
            device_id_type=MESH,
        )

    y_order = (4, 5, 2, 3, 6, 7, 1)

    for chunk in range(CHUNKS):
        contribution(chunk)
        if chunk == 0:
            pl.semaphore_wait(barrier, 15 + far)
            for slot in y_order:
                tag_copy(slot).start()
        for slot in y_order:
            y_copy(chunk, slot).start()

    for chunk in range(CHUNKS):
        if chunk == 0:
            for slot in range(1, PIECES):
                tag_copy(slot).wait_recv()
        y_in[chunk, 0] = y_out[chunk, core * 4 + y]
        for slot in range(1, PIECES):
            y_copy(chunk, slot).wait_recv()
        tags = [tag_in[slot] for slot in range(PIECES)]
        for row in range(0, STEP, 8):
            for column in range(0, B, 128):
                spot = (slice(row, row + 8), slice(column, column + 128))
                blocks = [y_in[(chunk, slot) + spot] for slot in range(PIECES)]
                for target in range(TARGETS):
                    parts = [jnp.where(t == target, b, 0.0) for t, b in zip(tags, blocks)]
                    while len(parts) > 1:
                        parts = [a + b for a, b in zip(parts[::2], parts[1::2])]
                    x_out[(chunk, PLACE[target]) + spot] = parts[0]
        for shift in (2, 1, 3):
            x_copy(chunk, shift).start()

    for chunk in range(CHUNKS):
        for shift in range(1, 4):
            x_copy(chunk, shift).wait_recv()
        for q in range(2):
            first = [x_in[chunk, SHIFT_START[s] - 4 + q] for s in (1, 2, 3)]
            second = [x_in[chunk, 2 + q], x_in[chunk, 6] if q == 0 else None]
            near = [x >= s for s in (1, 2, 3)]
            sums = [x_out[chunk, q], x_out[chunk, 2 + q], jnp.zeros((STEP, B), F32)]
            for is_near, block in zip(near, first):
                sums[0] += jnp.where(is_near, block, 0.0)
                sums[1] += jnp.where(is_near, 0.0, block)
            for is_near, block in zip(near, second):
                if block is not None:
                    sums[1] += jnp.where(is_near, block, 0.0)
                    sums[2] += jnp.where(is_near, 0.0, block)
            for ahead in range(3):
                z_out[chunk, ahead, q] = sums[ahead]

        for ahead, other in ((0, 0), (0, 1), (1, 0), (1, 1), (2, 0), (2, 1)):
            if ahead == 0 and other == 0:

                @pl.when(far == 1)
                def _():
                    z_copy(chunk, 0, 0).start()

                @pl.when(far == 0)
                def _():
                    z_in[chunk, 0] = z_out[chunk, 0, core]
            else:
                z_copy(chunk, ahead, other).start()

    for chunk in range(CHUNKS):
        for slot in range(6):
            if slot == 0:

                @pl.when(far == 1)
                def _():
                    z_arrival(chunk, 0).wait_recv()
            else:
                z_arrival(chunk, slot).wait_recv()
        blocks = [z_in[chunk, slot] for slot in range(6)]
        total = (blocks[0] + blocks[1]) + (blocks[2] + blocks[3]) + (blocks[4] + blocks[5])
        rows_ = term * ROWS + chunk * STEP + lax.broadcasted_iota(jnp.int32, (STEP, B), 0)
        cols_ = lax.broadcasted_iota(jnp.int32, (STEP, B), 1)
        out[chunk * STEP : (chunk + 1) * STEP, :] = jnp.where((rows_ < left_dims[0]) & (cols_ < right_dims[0]), total, 0.0)

    for slot in range(1, PIECES):
        tag_copy(slot).wait_send()
    for chunk in range(CHUNKS):
        for slot in range(1, PIECES):
            y_copy(chunk, slot).wait_send()
        for shift in range(1, 4):
            x_copy(chunk, shift).wait_send()
        for ahead in range(3):
            for other in range(2):
                if ahead == 0 and other == 0:

                    @pl.when(far == 1)
                    def _():
                        z_copy(chunk, 0, 0).wait_send()
                else:
                    z_copy(chunk, ahead, other).wait_send()


def on_device(wavefunction, left_dims, right_dims, left_operators, right_operators, charges):
    smem = pl.BlockSpec(memory_space=pltpu.SMEM)
    hbm = pl.BlockSpec(memory_space=pl.ANY)
    dma = pltpu.SemaphoreType.DMA
    summed = pl.pallas_call(
        kernel,
        out_shape=jax.ShapeDtypeStruct((ROWS, B), F32),
        in_specs=[smem, smem, smem, hbm, hbm, hbm],
        out_specs=pl.BlockSpec(memory_space=pltpu.VMEM),
        scratch_shapes=[
            pltpu.VMEM((B, B), F32),
            pltpu.VMEM((PIECES, ROWS, B), F32),
            pltpu.VMEM((B, B), F32),
            pltpu.VMEM((8, 128), jnp.int32),
            pltpu.VMEM((PIECES, 8, 128), jnp.int32),
            pltpu.VMEM((CHUNKS, PIECES, STEP, B), F32),
            pltpu.VMEM((CHUNKS, PIECES, STEP, B), F32),
            pltpu.VMEM((CHUNKS, TARGETS, STEP, B), F32),
            pltpu.VMEM((CHUNKS, TARGETS - 4, STEP, B), F32),
            pltpu.VMEM((CHUNKS, 3, 2, STEP, B), F32),
            pltpu.VMEM((CHUNKS, 6, STEP, B), F32),
            dma((3,)),
            dma((PIECES,)),
            dma((PIECES,)),
            dma((CHUNKS, PIECES)),
            dma((CHUNKS, PIECES)),
            dma((CHUNKS, 4)),
            dma((CHUNKS, 4)),
            dma((CHUNKS, 6)),
            dma((CHUNKS, 6)),
        ],
        compiler_params=pltpu.CompilerParams(collective_id=0, has_side_effects=True, vmem_limit_bytes=24 << 20),
        name="sector_scatter",
    )(
        left_dims,
        right_dims,
        charges,
        pltpu.with_memory_space_constraint(wavefunction[0], pltpu.HBM),
        pltpu.with_memory_space_constraint(left_operators.reshape(PIECES, ROWS, B), pltpu.HBM),
        pltpu.with_memory_space_constraint(right_operators[0, 0], pltpu.HBM),
    )
    return summed[None]


def solution(mesh):
    in_specs = (
        P("op", None, None),
        P("op"),
        P("op"),
        P("op", "term", None, None),
        P("op", "term", None, None),
        P("op", "term"),
    )
    out_specs = P("op", "term", None)
    return jax.shard_map(
        on_device, mesh=mesh, in_specs=in_specs, out_specs=out_specs, check_vma=False
    )
```

```python
import functools

import jax
import jax.numpy as jnp
from jax import lax
from jax.experimental import pallas as pl
from jax.experimental.pallas import tpu as pltpu
from jax.sharding import PartitionSpec as P

B = 384
ROWS = 48
PIECES = 8
CHUNKS = 3
STEP = ROWS // CHUNKS
SUB = STEP // 4
SOURCES = 32
TARGETS = 19
MESH = pl.DeviceIdType.MESH
F32, BF16 = jnp.float32, jnp.bfloat16


def halves(value):
    high = value.astype(BF16)
    return high, (value - high.astype(F32)).astype(BF16)


def dot3(a, b, contract):
    dims = (contract, ((), ()))
    one = functools.partial(lax.dot_general, dimension_numbers=dims, preferred_element_type=F32)
    return one(a[0], b[0]) + (one(a[0], b[1]) + one(a[1], b[0]))


def kernel(
    left_dims, right_dims, charges, wave_hbm, left_hbm, right_hbm, out,
    wave, left, right, tag_out, tag_in, plane_out, plane_in, deep_out, deep_in,
    in_sem, tag_ss, tag_rs, plane_ss, plane_rs, deep_ss, deep_rs, last_rs,
):
    op, term = lax.axis_index("op"), lax.axis_index("term")
    core, x, z_lo = op % 2, (op // 2) % 4, op // 8
    y, z_hi = term % 4, term // 4
    far = (z_hi + core) % 2
    local = 2 * x + core
    mine = local * 4 + y

    def device(z_lo_, x_, core_, z_hi_, y_):
        return {"op": (z_lo_ * 4 + x_) * 2 + core_, "term": z_hi_ * 4 + y_}

    loads = [
        pltpu.make_async_copy(wave_hbm, wave, in_sem.at[0]),
        pltpu.make_async_copy(left_hbm, left, in_sem.at[1]),
        pltpu.make_async_copy(right_hbm, right, in_sem.at[2]),
    ]
    for load in loads:
        load.start()

    barrier = pltpu.get_barrier_semaphore()

    def greet(device_id):
        pl.semaphore_signal(barrier, inc=1, device_id=device_id, device_id_type=MESH)

    steps = [(dx, dy, dc) for dx in (2, 1, 3, 0) for dy in (2, 1, 3, 0) for dc in (0, 1)][:-2] + [(0, 0, 1)]

    def plane_peer(step):
        dx, dy, dc = step
        return (x + dx) % 4, (y + dy) % 4, (core + dc) % 2

    for ahead, half in ((1, 0), (1, 1), (0, 1)):
        for x_ in range(4):
            greet(device((z_lo + 4 - ahead) % 4, x_, z_hi, (z_hi + half) % 2, y))

    @pl.when(local < TARGETS - 16)
    def _():
        for half in range(2):
            for x_ in range(4):
                greet(device((z_lo + 2) % 4, x_, z_hi, (z_hi + half) % 2, y))

    for step in steps:
        x_, y_, core_ = plane_peer(step)
        greet(device(z_lo, x_, core_, z_hi, y_))

    tag_out[...] = jnp.full((1, 128), charges[0, 0] + local, jnp.int32)
    tag_in[mine] = tag_out[...]

    loads[0].wait()
    live = (lax.broadcasted_iota(jnp.int32, (B, B), 0) < left_dims[0]) & (
        lax.broadcasted_iota(jnp.int32, (B, B), 1) < right_dims[0]
    )
    wave_parts = halves(jnp.where(live, wave[...], 0.0))
    loads[2].wait()
    right_parts = halves(right[...])
    loads[1].wait()

    def contribution(chunk):
        rows = left[:, chunk * STEP : (chunk + 1) * STEP, :].reshape(PIECES * STEP, B)
        product = dot3(halves(rows), wave_parts, ((1,), (0,)))
        result = dot3(halves(product), right_parts, ((1,), (1,)))
        for piece in range(PIECES):
            for place in range(4):
                row = piece * STEP + place * SUB
                plane_out[chunk, piece, place] = result[row : row + SUB]

    def plane_copy(chunk, step):
        x_, y_, core_ = plane_peer(step)
        return pltpu.make_async_remote_copy(
            src_ref=plane_out.at[chunk, core_ * 4 + y_, x_],
            dst_ref=plane_in.at[chunk, mine],
            send_sem=plane_ss.at[chunk],
            recv_sem=plane_rs.at[chunk],
            device_id=device(z_lo, x_, core_, z_hi, y_),
            device_id_type=MESH,
        )

    def tag_copy(step):
        x_, y_, core_ = plane_peer(step)
        return pltpu.make_async_remote_copy(
            src_ref=tag_out,
            dst_ref=tag_in.at[mine],
            send_sem=tag_ss,
            recv_sem=tag_rs,
            device_id=device(z_lo, x_, core_, z_hi, y_),
            device_id_type=MESH,
        )

    def bulk(source, target, send_sem, recv_sem):
        return pltpu.make_async_remote_copy(
            src_ref=source,
            dst_ref=target,
            send_sem=send_sem,
            recv_sem=recv_sem,
            device_id=device(z_lo, x, (core + 1) % 2, z_hi, y),
            device_id_type=MESH,
        )

    def deep_copy(chunk, ahead, x_, core_, recv_sem):
        return pltpu.make_async_remote_copy(
            src_ref=deep_out.at[chunk, ahead * 8 + x_ * 2 + core_],
            dst_ref=deep_in.at[chunk, ahead * 2 + far, x],
            send_sem=deep_ss.at[chunk],
            recv_sem=recv_sem,
            device_id=device((z_lo + ahead) % 4, x_, core_, core, y),
            device_id_type=MESH,
        )

    for chunk in range(CHUNKS):
        contribution(chunk)
        if chunk == 0:
            pl.semaphore_wait(barrier, 42 + 8 * far)
            for step in steps:
                tag_copy(step).start()
        for step in steps:
            plane_copy(chunk, step).start()
        plane_in[chunk, mine] = plane_out[chunk, core * 4 + y, x]

    everyone = pl.ds(0, SOURCES - 1)
    for chunk in range(CHUNKS):
        if chunk == 0:
            bulk(tag_in.at[everyone], tag_in.at[everyone], tag_ss, tag_rs).wait_recv()
        bulk(
            plane_in.at[chunk, everyone], plane_in.at[chunk, everyone], plane_ss.at[chunk], plane_rs.at[chunk]
        ).wait_recv()
        for column in range(0, B, 128):
            columns = slice(column, column + 128)
            sums = [None] * TARGETS
            for source in range(SOURCES):
                tag = jnp.broadcast_to(tag_in[source], (SUB, 128))
                block = plane_in[chunk, source, :, columns]
                for target in range(source // 4, source // 4 + 12):
                    part = jnp.where(tag == target, block, 0.0)
                    sums[target] = part if sums[target] is None else sums[target] + part
            for target in range(TARGETS):
                deep_out[chunk, target, :, columns] = sums[target]

        for ahead in (1, 2, 0):
            if ahead == 2:
                for target in range(TARGETS - 16):
                    deep_copy(chunk, 2, target // 2, target % 2, last_rs.at[chunk]).start()
                continue
            for dx in (2, 1, 3, 0):
                for dc in range(2):
                    x_, core_ = (x + dx) % 4, (core + dc) % 2
                    send = functools.partial(
                        lambda *a: deep_copy(*a).start(), chunk, ahead, x_, core_, deep_rs.at[chunk]
                    )
                    if ahead or dx or dc:
                        send()
                    else:
                        pl.when(far == 1)(send)

                        @pl.when(far == 0)
                        def _():
                            deep_in[chunk, 0, x] = deep_out[chunk, local]

    for chunk in range(CHUNKS):

        @pl.when(far == 1)
        def _():
            both = deep_in.at[chunk, pl.ds(0, 4)]
            bulk(both, both, deep_ss.at[chunk], deep_rs.at[chunk]).wait_recv()

        @pl.when(far == 0)
        def _():
            most = plane_in.at[chunk, pl.ds(0, 15)]
            bulk(most, most, deep_ss.at[chunk], deep_rs.at[chunk]).wait_recv()

        def limited(value, place):
            row = term * ROWS + chunk * STEP + place * SUB + lax.broadcasted_iota(jnp.int32, (SUB, B), 0)
            column = lax.broadcasted_iota(jnp.int32, (SUB, B), 1)
            return jnp.where((row < left_dims[0]) & (column < right_dims[0]), value, 0.0)

        def total(slots, place):
            value = deep_in[chunk, slots[0], place]
            for slot in slots[1:]:
                value += deep_in[chunk, slot, place]
            return value

        def spot(place):
            start = chunk * STEP + place * SUB
            return slice(start, start + SUB)

        @pl.when(local < TARGETS - 16)
        def _():
            rest = deep_in.at[chunk, pl.ds(4, 2)]
            bulk(rest, rest, deep_ss.at[chunk], last_rs.at[chunk]).wait_recv()
            for place in range(4):
                out[spot(place), :] = limited(total(range(6), place), place)

        @pl.when(local >= TARGETS - 16)
        def _():
            for place in range(4):
                out[spot(place), :] = limited(total(range(4), place), place)

    bulk(tag_in.at[everyone], tag_in.at[everyone], tag_ss, tag_rs).wait_send()
    for chunk in range(CHUNKS):
        bulk(
            plane_in.at[chunk, everyone], plane_in.at[chunk, everyone], plane_ss.at[chunk], plane_rs.at[chunk]
        ).wait_send()

        @pl.when(far == 1)
        def _():
            bulk(deep_out.at[chunk], deep_out.at[chunk], deep_ss.at[chunk], deep_rs.at[chunk]).wait_send()

        @pl.when(far == 0)
        def _():
            most = deep_out.at[chunk, pl.ds(0, TARGETS - 1)]
            bulk(most, most, deep_ss.at[chunk], deep_rs.at[chunk]).wait_send()


def on_device(wavefunction, left_dims, right_dims, left_operators, right_operators, charges):
    smem = pl.BlockSpec(memory_space=pltpu.SMEM)
    hbm = pl.BlockSpec(memory_space=pl.ANY)
    dma = pltpu.SemaphoreType.DMA
    summed = pl.pallas_call(
        kernel,
        out_shape=jax.ShapeDtypeStruct((ROWS, B), F32),
        in_specs=[smem, smem, smem, hbm, hbm, hbm],
        out_specs=pl.BlockSpec(memory_space=pltpu.VMEM),
        scratch_shapes=[
            pltpu.VMEM((B, B), F32),
            pltpu.VMEM((PIECES, ROWS, B), F32),
            pltpu.VMEM((B, B), F32),
            pltpu.VMEM((1, 128), jnp.int32),
            pltpu.VMEM((SOURCES, 1, 128), jnp.int32),
            pltpu.VMEM((CHUNKS, PIECES, 4, SUB, B), F32),
            pltpu.VMEM((CHUNKS, SOURCES, SUB, B), F32),
            pltpu.VMEM((CHUNKS, TARGETS, SUB, B), F32),
            pltpu.VMEM((CHUNKS, 6, 4, SUB, B), F32),
            dma((3,)),
            dma(()),
            dma(()),
            dma((CHUNKS,)),
            dma((CHUNKS,)),
            dma((CHUNKS,)),
            dma((CHUNKS,)),
            dma((CHUNKS,)),
        ],
        compiler_params=pltpu.CompilerParams(
            collective_id=0, has_side_effects=True, vmem_limit_bytes=24 << 20
        ),
        name="sector_scatter",
    )(
        left_dims,
        right_dims,
        charges,
        pltpu.with_memory_space_constraint(wavefunction[0], pltpu.HBM),
        pltpu.with_memory_space_constraint(left_operators.reshape(PIECES, ROWS, B), pltpu.HBM),
        pltpu.with_memory_space_constraint(right_operators[0, 0], pltpu.HBM),
    )
    return summed[None]


def solution(mesh):
    in_specs = (
        P("op", None, None),
        P("op"),
        P("op"),
        P("op", "term", None, None),
        P("op", "term", None, None),
        P("op", "term"),
    )
    out_specs = P("op", "term", None)
    return jax.shard_map(
        on_device, mesh=mesh, in_specs=in_specs, out_specs=out_specs, check_vma=False
    )
```

```python
import functools

import jax
import jax.numpy as jnp
from jax import lax
from jax.experimental import pallas as pl
from jax.experimental.pallas import tpu as pltpu
from jax.sharding import PartitionSpec as P

B = 384
ROWS = 48
PIECES = 8
STEP = 16
SUB = STEP // 4
CHUNKS = ((0, 0, 128), (0, 128, 128), (0, 256, 128), (1, 0, 384), (2, 0, 384))
SOURCES = 32
TARGETS = 19
MESH = pl.DeviceIdType.MESH
F32, BF16 = jnp.float32, jnp.bfloat16


def halves(value):
    high = value.astype(BF16)
    return high, (value - high.astype(F32)).astype(BF16)


def dot3(a, b, contract):
    dims = (contract, ((), ()))
    one = functools.partial(lax.dot_general, dimension_numbers=dims, preferred_element_type=F32)
    return one(a[0], b[0]) + (one(a[0], b[1]) + one(a[1], b[0]))


def kernel(
    left_dims, right_dims, charges, wave_hbm, left_hbm, right_hbm, out,
    wave, left, right, tag_out, tag_in, plane_out, plane_in, deep_out, deep_in,
    in_sem, tag_ss, tag_rs, plane_ss, plane_rs, deep_ss, deep_rs, last_rs,
):
    op, term = lax.axis_index("op"), lax.axis_index("term")
    core, x, z_lo = op % 2, (op // 2) % 4, op // 8
    y, z_hi = term % 4, term // 4
    far = (z_hi + core) % 2
    local = 2 * x + core
    mine = local * 4 + y

    def device(z_lo_, x_, core_, z_hi_, y_):
        return {"op": (z_lo_ * 4 + x_) * 2 + core_, "term": z_hi_ * 4 + y_}

    def left_load(block):
        rows = pl.ds(block * STEP, STEP)
        return pltpu.make_async_copy(left_hbm.at[:, rows], left.at[:, rows], in_sem.at[1 + block])

    def right_load(chunk):
        rows = pl.ds(CHUNKS[chunk][1], CHUNKS[chunk][2])
        return pltpu.make_async_copy(right_hbm.at[rows], right.at[rows], in_sem.at[4 + chunk])

    wave_load = pltpu.make_async_copy(wave_hbm, wave, in_sem.at[0])
    right_loads = [right_load(chunk) for chunk in range(len(CHUNKS)) if CHUNKS[chunk][0] == 0]
    for load in (wave_load, left_load(0), *right_loads, left_load(1), left_load(2)):
        load.start()

    barrier = pltpu.get_barrier_semaphore()

    def greet(device_id):
        pl.semaphore_signal(barrier, inc=1, device_id=device_id, device_id_type=MESH)

    steps = [(dx, dy, dc) for dx in (2, 1, 3, 0) for dy in (2, 1, 3, 0) for dc in (0, 1)][:-2] + [(0, 0, 1)]

    def plane_peer(step):
        dx, dy, dc = step
        return (x + dx) % 4, (y + dy) % 4, (core + dc) % 2

    for ahead, half in ((1, 0), (1, 1), (0, 1)):
        for x_ in range(4):
            greet(device((z_lo + 4 - ahead) % 4, x_, z_hi, (z_hi + half) % 2, y))

    @pl.when(local < TARGETS - 16)
    def _():
        for half in range(2):
            for x_ in range(4):
                greet(device((z_lo + 2) % 4, x_, z_hi, (z_hi + half) % 2, y))

    for step in steps:
        x_, y_, core_ = plane_peer(step)
        greet(device(z_lo, x_, core_, z_hi, y_))

    tag_out[...] = jnp.full((1, 128), charges[0, 0] + local, jnp.int32)
    tag_in[mine] = tag_out[...]

    wave_load.wait()
    live = (lax.broadcasted_iota(jnp.int32, (B, B), 0) < left_dims[0]) & (
        lax.broadcasted_iota(jnp.int32, (B, B), 1) < right_dims[0]
    )
    wave_parts = halves(jnp.where(live, wave[...], 0.0))
    products, right_parts = {}, {}

    def contribution(chunk):
        block, start, width = CHUNKS[chunk]
        if block not in products:
            left_load(block).wait()
            rows = left[:, block * STEP : (block + 1) * STEP, :].reshape(PIECES * STEP, B)
            products[block] = halves(dot3(halves(rows), wave_parts, ((1,), (0,))))
        if block == 0:
            right_load(chunk).wait()
            right_parts[start] = halves(right[start : start + width])
        for first, part in right_parts.items():
            if start <= first < start + width:
                result = dot3(products[block], part, ((1,), (1,)))
                columns = slice(first - start, first - start + part[0].shape[0])
                for piece in range(PIECES):
                    for place in range(4):
                        row = piece * STEP + place * SUB
                        plane_out[chunk][piece, place, :, columns] = result[row : row + SUB]

    def plane_copy(chunk, step):
        x_, y_, core_ = plane_peer(step)
        return pltpu.make_async_remote_copy(
            src_ref=plane_out[chunk].at[core_ * 4 + y_, x_],
            dst_ref=plane_in[chunk].at[mine],
            send_sem=plane_ss.at[chunk],
            recv_sem=plane_rs.at[chunk],
            device_id=device(z_lo, x_, core_, z_hi, y_),
            device_id_type=MESH,
        )

    def tag_copy(step):
        x_, y_, core_ = plane_peer(step)
        return pltpu.make_async_remote_copy(
            src_ref=tag_out,
            dst_ref=tag_in.at[mine],
            send_sem=tag_ss,
            recv_sem=tag_rs,
            device_id=device(z_lo, x_, core_, z_hi, y_),
            device_id_type=MESH,
        )

    def bulk(source, target, send_sem, recv_sem):
        return pltpu.make_async_remote_copy(
            src_ref=source,
            dst_ref=target,
            send_sem=send_sem,
            recv_sem=recv_sem,
            device_id=device(z_lo, x, (core + 1) % 2, z_hi, y),
            device_id_type=MESH,
        )

    def deep_copy(chunk, ahead, x_, core_, recv_sem):
        return pltpu.make_async_remote_copy(
            src_ref=deep_out[chunk].at[ahead * 8 + x_ * 2 + core_],
            dst_ref=deep_in[chunk].at[ahead * 2 + far, x],
            send_sem=deep_ss.at[chunk],
            recv_sem=recv_sem,
            device_id=device((z_lo + ahead) % 4, x_, core_, core, y),
            device_id_type=MESH,
        )

    for chunk in range(len(CHUNKS)):
        contribution(chunk)
        if chunk == 0:
            pl.semaphore_wait(barrier, 42 + 8 * far)
            for step in steps:
                tag_copy(step).start()
        for step in steps:
            plane_copy(chunk, step).start()
        plane_in[chunk][mine] = plane_out[chunk][core * 4 + y, x]

    everyone = pl.ds(0, SOURCES - 1)
    for chunk in range(len(CHUNKS)):
        if chunk == 0:
            bulk(tag_in.at[everyone], tag_in.at[everyone], tag_ss, tag_rs).wait_recv()
        bulk(
            plane_in[chunk].at[everyone], plane_in[chunk].at[everyone], plane_ss.at[chunk], plane_rs.at[chunk]
        ).wait_recv()
        for column in range(0, CHUNKS[chunk][2], 128):
            columns = slice(column, column + 128)
            sums = [None] * TARGETS
            for source in range(SOURCES):
                tag = jnp.broadcast_to(tag_in[source], (SUB, 128))
                block = plane_in[chunk][source, :, columns]
                for target in range(source // 4, source // 4 + 12):
                    part = jnp.where(tag == target, block, 0.0)
                    sums[target] = part if sums[target] is None else sums[target] + part
            for target in range(TARGETS):
                deep_out[chunk][target, :, columns] = sums[target]

        for ahead in (1, 2, 0):
            if ahead == 2:
                for target in range(TARGETS - 16):
                    deep_copy(chunk, 2, target // 2, target % 2, last_rs.at[chunk]).start()
                continue
            for dx in (2, 1, 3, 0):
                for dc in range(2):
                    x_, core_ = (x + dx) % 4, (core + dc) % 2
                    send = functools.partial(
                        lambda *a: deep_copy(*a).start(), chunk, ahead, x_, core_, deep_rs.at[chunk]
                    )
                    if ahead or dx or dc:
                        send()
                    else:
                        pl.when(far == 1)(send)

                        @pl.when(far == 0)
                        def _():
                            deep_in[chunk][0, x] = deep_out[chunk][local]

    for chunk in range(len(CHUNKS)):

        @pl.when(far == 1)
        def _():
            both = deep_in[chunk].at[pl.ds(0, 4)]
            bulk(both, both, deep_ss.at[chunk], deep_rs.at[chunk]).wait_recv()

        @pl.when(far == 0)
        def _():
            most = plane_in[chunk].at[pl.ds(0, 15)]
            bulk(most, most, deep_ss.at[chunk], deep_rs.at[chunk]).wait_recv()

        block, start, width = CHUNKS[chunk]

        def limited(value, place):
            row = term * ROWS + block * STEP + place * SUB + lax.broadcasted_iota(jnp.int32, (SUB, width), 0)
            column = start + lax.broadcasted_iota(jnp.int32, (SUB, width), 1)
            return jnp.where((row < left_dims[0]) & (column < right_dims[0]), value, 0.0)

        def total(slots, place):
            value = deep_in[chunk][slots[0], place]
            for slot in slots[1:]:
                value += deep_in[chunk][slot, place]
            return value

        def spot(place):
            row = block * STEP + place * SUB
            return slice(row, row + SUB), slice(start, start + width)

        @pl.when(local < TARGETS - 16)
        def _():
            rest = deep_in[chunk].at[pl.ds(4, 2)]
            bulk(rest, rest, deep_ss.at[chunk], last_rs.at[chunk]).wait_recv()
            for place in range(4):
                out[spot(place)] = limited(total(range(6), place), place)

        @pl.when(local >= TARGETS - 16)
        def _():
            for place in range(4):
                out[spot(place)] = limited(total(range(4), place), place)

    bulk(tag_in.at[everyone], tag_in.at[everyone], tag_ss, tag_rs).wait_send()
    for chunk in range(len(CHUNKS)):
        bulk(
            plane_in[chunk].at[everyone], plane_in[chunk].at[everyone], plane_ss.at[chunk], plane_rs.at[chunk]
        ).wait_send()

        @pl.when(far == 1)
        def _():
            bulk(deep_out[chunk], deep_out[chunk], deep_ss.at[chunk], deep_rs.at[chunk]).wait_send()

        @pl.when(far == 0)
        def _():
            most = deep_out[chunk].at[pl.ds(0, TARGETS - 1)]
            bulk(most, most, deep_ss.at[chunk], deep_rs.at[chunk]).wait_send()


def on_device(wavefunction, left_dims, right_dims, left_operators, right_operators, charges):
    smem = pl.BlockSpec(memory_space=pltpu.SMEM)
    hbm = pl.BlockSpec(memory_space=pl.ANY)
    dma = pltpu.SemaphoreType.DMA

    def per_chunk(*leading):
        return [pltpu.VMEM((*leading, SUB, width), F32) for _, _, width in CHUNKS]

    summed = pl.pallas_call(
        kernel,
        out_shape=jax.ShapeDtypeStruct((ROWS, B), F32),
        in_specs=[smem, smem, smem, hbm, hbm, hbm],
        out_specs=pl.BlockSpec(memory_space=pltpu.VMEM),
        scratch_shapes=[
            pltpu.VMEM((B, B), F32),
            pltpu.VMEM((PIECES, ROWS, B), F32),
            pltpu.VMEM((B, B), F32),
            pltpu.VMEM((1, 128), jnp.int32),
            pltpu.VMEM((SOURCES, 1, 128), jnp.int32),
            per_chunk(PIECES, 4),
            per_chunk(SOURCES),
            per_chunk(TARGETS),
            per_chunk(6, 4),
            dma((4 + len(CHUNKS),)),
            dma(()),
            dma(()),
            dma((len(CHUNKS),)),
            dma((len(CHUNKS),)),
            dma((len(CHUNKS),)),
            dma((len(CHUNKS),)),
            dma((len(CHUNKS),)),
        ],
        compiler_params=pltpu.CompilerParams(
            collective_id=0, has_side_effects=True, vmem_limit_bytes=24 << 20
        ),
        name="sector_scatter",
    )(
        left_dims,
        right_dims,
        charges,
        pltpu.with_memory_space_constraint(wavefunction[0], pltpu.HBM),
        pltpu.with_memory_space_constraint(left_operators.reshape(PIECES, ROWS, B), pltpu.HBM),
        pltpu.with_memory_space_constraint(right_operators[0, 0], pltpu.HBM),
    )
    return summed[None]


def solution(mesh):
    in_specs = (
        P("op", None, None),
        P("op"),
        P("op"),
        P("op", "term", None, None),
        P("op", "term", None, None),
        P("op", "term"),
    )
    out_specs = P("op", "term", None)
    return jax.shard_map(
        on_device, mesh=mesh, in_specs=in_specs, out_specs=out_specs, check_vma=False
    )
```

```python
import functools

import jax
import jax.numpy as jnp
from jax import lax
from jax.experimental import pallas as pl
from jax.experimental.pallas import tpu as pltpu
from jax.sharding import PartitionSpec as P

B = 384
ROWS = 48
PIECES = 8
STEP = 16
SUB = STEP // 4
CHUNKS = ((0, 0, 128), (0, 128, 128), (0, 256, 128), (1, 0, 384), (2, 0, 384))
SOURCES = 32
TARGETS = 19
MESH = pl.DeviceIdType.MESH
F32, BF16 = jnp.float32, jnp.bfloat16


def halves(value):
    high = value.astype(BF16)
    return high, (value - high.astype(F32)).astype(BF16)


def dot3(a, b, contract):
    dims = (contract, ((), ()))
    one = functools.partial(lax.dot_general, dimension_numbers=dims, preferred_element_type=F32)
    return one(a[0], b[0]) + (one(a[0], b[1]) + one(a[1], b[0]))


def kernel(
    left_dims, right_dims, charges, wave_hbm, left_hbm, right_hbm, out,
    wave, left, right, tag_out, tag_in, plane_out, plane_in, deep_out, deep_in,
    in_sem, tag_ss, tag_rs, plane_ss, plane_rs, deep_ss, deep_rs, last_rs,
):
    op, term = lax.axis_index("op"), lax.axis_index("term")
    core, x, z_lo = op % 2, (op // 2) % 4, op // 8
    y, z_hi = term % 4, term // 4
    far = (z_hi + core) % 2
    local = 2 * x + core
    mine = local * 4 + y

    def device(z_lo_, x_, core_, z_hi_, y_):
        return {"op": (z_lo_ * 4 + x_) * 2 + core_, "term": z_hi_ * 4 + y_}

    def left_load(block):
        rows = pl.ds(block * STEP, STEP)
        return pltpu.make_async_copy(left_hbm.at[:, rows], left.at[:, rows], in_sem.at[1 + block])

    def right_load(chunk):
        rows = pl.ds(CHUNKS[chunk][1], CHUNKS[chunk][2])
        return pltpu.make_async_copy(right_hbm.at[rows], right.at[rows], in_sem.at[4 + chunk])

    wave_load = pltpu.make_async_copy(wave_hbm, wave, in_sem.at[0])
    right_loads = [right_load(chunk) for chunk in range(len(CHUNKS)) if CHUNKS[chunk][0] == 0]
    for load in (wave_load, left_load(0), *right_loads, left_load(1), left_load(2)):
        load.start()

    barrier = pltpu.get_barrier_semaphore()

    def greet(device_id):
        pl.semaphore_signal(barrier, inc=1, device_id=device_id, device_id_type=MESH)

    places = [(dx, dy) for dx in (2, 1, 3, 0) for dy in (2, 1, 3, 0)][:-1]
    to_first, to_second = ([(dx, dy, core_) for dx, dy in places] for core_ in range(2))
    beside = [(0, 0, (core + 1) % 2)]
    steps = [*to_first, *to_second, *beside]

    def plane_peer(step):
        dx, dy, core_ = step
        return (x + dx) % 4, (y + dy) % 4, core_

    for ahead, half in ((1, 0), (1, 1), (0, 1)):
        for x_ in range(4):
            greet(device((z_lo + 4 - ahead) % 4, x_, z_hi, (z_hi + half) % 2, y))

    @pl.when(local < TARGETS - 16)
    def _():
        for half in range(2):
            for x_ in range(4):
                greet(device((z_lo + 2) % 4, x_, z_hi, (z_hi + half) % 2, y))

    for step in steps:
        x_, y_, core_ = plane_peer(step)
        greet(device(z_lo, x_, core_, z_hi, y_))

    tag_out[...] = jnp.full((1, 128), charges[0, 0] + local, jnp.int32)
    tag_in[mine] = tag_out[...]

    wave_load.wait()
    live = (lax.broadcasted_iota(jnp.int32, (B, B), 0) < left_dims[0]) & (
        lax.broadcasted_iota(jnp.int32, (B, B), 1) < right_dims[0]
    )
    wave_parts = halves(jnp.where(live, wave[...], 0.0))
    products, right_parts = {}, {}

    def contribution(chunk):
        block, start, width = CHUNKS[chunk]
        if block not in products:
            left_load(block).wait()
            rows = left[:, block * STEP : (block + 1) * STEP, :].reshape(PIECES * STEP, B)
            products[block] = halves(dot3(halves(rows), wave_parts, ((1,), (0,))))
        if block == 0:
            right_load(chunk).wait()
            right_parts[start] = halves(right[start : start + width])
        for first, part in right_parts.items():
            if start <= first < start + width:
                result = dot3(products[block], part, ((1,), (1,)))
                columns = slice(first - start, first - start + part[0].shape[0])
                for piece in range(PIECES):
                    for place in range(4):
                        row = piece * STEP + place * SUB
                        plane_out[chunk][piece, place, :, columns] = result[row : row + SUB]

    def plane_copy(chunk, step):
        x_, y_, core_ = plane_peer(step)
        return pltpu.make_async_remote_copy(
            src_ref=plane_out[chunk].at[core_ * 4 + y_, x_],
            dst_ref=plane_in[chunk].at[mine],
            send_sem=plane_ss.at[chunk],
            recv_sem=plane_rs.at[chunk],
            device_id=device(z_lo, x_, core_, z_hi, y_),
            device_id_type=MESH,
        )

    def tag_copy(step):
        x_, y_, core_ = plane_peer(step)
        return pltpu.make_async_remote_copy(
            src_ref=tag_out,
            dst_ref=tag_in.at[mine],
            send_sem=tag_ss,
            recv_sem=tag_rs,
            device_id=device(z_lo, x_, core_, z_hi, y_),
            device_id_type=MESH,
        )

    def bulk(source, target, send_sem, recv_sem):
        return pltpu.make_async_remote_copy(
            src_ref=source,
            dst_ref=target,
            send_sem=send_sem,
            recv_sem=recv_sem,
            device_id=device(z_lo, x, (core + 1) % 2, z_hi, y),
            device_id_type=MESH,
        )

    def deep_copy(chunk, ahead, x_, core_, recv_sem):
        return pltpu.make_async_remote_copy(
            src_ref=deep_out[chunk].at[ahead * 8 + x_ * 2 + core_],
            dst_ref=deep_in[chunk].at[ahead * 2 + far, x],
            send_sem=deep_ss.at[chunk],
            recv_sem=recv_sem,
            device_id=device((z_lo + ahead) % 4, x_, core_, core, y),
            device_id_type=MESH,
        )

    for chunk in range(len(CHUNKS)):
        contribution(chunk)
        if chunk == 0:
            pl.semaphore_wait(barrier, 42 + 8 * far)
            for step in steps:
                tag_copy(step).start()
        for step in (*to_first, *beside):
            plane_copy(chunk, step).start()
        if chunk > 1:
            for step in to_second:
                plane_copy(chunk - 2, step).start()
        plane_in[chunk][mine] = plane_out[chunk][core * 4 + y, x]

    for chunk in range(len(CHUNKS) - 2, len(CHUNKS)):
        for step in to_second:
            plane_copy(chunk, step).start()

    everyone = pl.ds(0, SOURCES - 1)
    for chunk in range(len(CHUNKS)):
        if chunk == 0:
            bulk(tag_in.at[everyone], tag_in.at[everyone], tag_ss, tag_rs).wait_recv()
        bulk(
            plane_in[chunk].at[everyone], plane_in[chunk].at[everyone], plane_ss.at[chunk], plane_rs.at[chunk]
        ).wait_recv()
        for column in range(0, CHUNKS[chunk][2], 128):
            columns = slice(column, column + 128)
            sums = [None] * TARGETS
            for source in range(SOURCES):
                tag = jnp.broadcast_to(tag_in[source], (SUB, 128))
                block = plane_in[chunk][source, :, columns]
                for target in range(source // 4, source // 4 + 12):
                    part = jnp.where(tag == target, block, 0.0)
                    sums[target] = part if sums[target] is None else sums[target] + part
            for target in range(TARGETS):
                deep_out[chunk][target, :, columns] = sums[target]

        for ahead in (1, 2, 0):
            if ahead == 2:
                for target in range(TARGETS - 16):
                    deep_copy(chunk, 2, target // 2, target % 2, last_rs.at[chunk]).start()
                continue
            for dx in (2, 1, 3, 0):
                for dc in range(2):
                    x_, core_ = (x + dx) % 4, (core + dc) % 2
                    send = functools.partial(
                        lambda *a: deep_copy(*a).start(), chunk, ahead, x_, core_, deep_rs.at[chunk]
                    )
                    if ahead or dx or dc:
                        send()
                    else:
                        pl.when(far == 1)(send)

                        @pl.when(far == 0)
                        def _():
                            deep_in[chunk][0, x] = deep_out[chunk][local]

    for chunk in range(len(CHUNKS)):

        @pl.when(far == 1)
        def _():
            both = deep_in[chunk].at[pl.ds(0, 4)]
            bulk(both, both, deep_ss.at[chunk], deep_rs.at[chunk]).wait_recv()

        @pl.when(far == 0)
        def _():
            most = plane_in[chunk].at[pl.ds(0, 15)]
            bulk(most, most, deep_ss.at[chunk], deep_rs.at[chunk]).wait_recv()

        block, start, width = CHUNKS[chunk]

        def limited(value, place):
            row = term * ROWS + block * STEP + place * SUB + lax.broadcasted_iota(jnp.int32, (SUB, width), 0)
            column = start + lax.broadcasted_iota(jnp.int32, (SUB, width), 1)
            return jnp.where((row < left_dims[0]) & (column < right_dims[0]), value, 0.0)

        def total(slots, place):
            value = deep_in[chunk][slots[0], place]
            for slot in slots[1:]:
                value += deep_in[chunk][slot, place]
            return value

        def spot(place):
            row = block * STEP + place * SUB
            return slice(row, row + SUB), slice(start, start + width)

        @pl.when(local < TARGETS - 16)
        def _():
            rest = deep_in[chunk].at[pl.ds(4, 2)]
            bulk(rest, rest, deep_ss.at[chunk], last_rs.at[chunk]).wait_recv()
            for place in range(4):
                out[spot(place)] = limited(total(range(6), place), place)

        @pl.when(local >= TARGETS - 16)
        def _():
            for place in range(4):
                out[spot(place)] = limited(total(range(4), place), place)

    bulk(tag_in.at[everyone], tag_in.at[everyone], tag_ss, tag_rs).wait_send()
    for chunk in range(len(CHUNKS)):
        bulk(
            plane_in[chunk].at[everyone], plane_in[chunk].at[everyone], plane_ss.at[chunk], plane_rs.at[chunk]
        ).wait_send()

        @pl.when(far == 1)
        def _():
            bulk(deep_out[chunk], deep_out[chunk], deep_ss.at[chunk], deep_rs.at[chunk]).wait_send()

        @pl.when(far == 0)
        def _():
            most = deep_out[chunk].at[pl.ds(0, TARGETS - 1)]
            bulk(most, most, deep_ss.at[chunk], deep_rs.at[chunk]).wait_send()


def on_device(wavefunction, left_dims, right_dims, left_operators, right_operators, charges):
    smem = pl.BlockSpec(memory_space=pltpu.SMEM)
    hbm = pl.BlockSpec(memory_space=pl.ANY)
    dma = pltpu.SemaphoreType.DMA

    def per_chunk(*leading):
        return [pltpu.VMEM((*leading, SUB, width), F32) for _, _, width in CHUNKS]

    summed = pl.pallas_call(
        kernel,
        out_shape=jax.ShapeDtypeStruct((ROWS, B), F32),
        in_specs=[smem, smem, smem, hbm, hbm, hbm],
        out_specs=pl.BlockSpec(memory_space=pltpu.VMEM),
        scratch_shapes=[
            pltpu.VMEM((B, B), F32),
            pltpu.VMEM((PIECES, ROWS, B), F32),
            pltpu.VMEM((B, B), F32),
            pltpu.VMEM((1, 128), jnp.int32),
            pltpu.VMEM((SOURCES, 1, 128), jnp.int32),
            per_chunk(PIECES, 4),
            per_chunk(SOURCES),
            per_chunk(TARGETS),
            per_chunk(6, 4),
            dma((4 + len(CHUNKS),)),
            dma(()),
            dma(()),
            dma((len(CHUNKS),)),
            dma((len(CHUNKS),)),
            dma((len(CHUNKS),)),
            dma((len(CHUNKS),)),
            dma((len(CHUNKS),)),
        ],
        compiler_params=pltpu.CompilerParams(
            collective_id=0, has_side_effects=True, vmem_limit_bytes=24 << 20
        ),
        name="sector_scatter",
    )(
        left_dims,
        right_dims,
        charges,
        pltpu.with_memory_space_constraint(wavefunction[0], pltpu.HBM),
        pltpu.with_memory_space_constraint(left_operators.reshape(PIECES, ROWS, B), pltpu.HBM),
        pltpu.with_memory_space_constraint(right_operators[0, 0], pltpu.HBM),
    )
    return summed[None]


def solution(mesh):
    in_specs = (
        P("op", None, None),
        P("op"),
        P("op"),
        P("op", "term", None, None),
        P("op", "term", None, None),
        P("op", "term"),
    )
    out_specs = P("op", "term", None)
    return jax.shard_map(
        on_device, mesh=mesh, in_specs=in_specs, out_specs=out_specs, check_vma=False
    )
```
